32 devices in a mesh: blk: 8 (over z, y), col: 4 (over x, core).
Axes of the slice: x: 2, y: 2, z: 4, core: 2. Of those that a mesh axis runs over, the one named last changes fastest.
Arguments:
- direct_init: float32 [5, 8, 4096], P(None, 'col', 'blk'), may hold values from -6 to 6
- adjoint_init: float32 [5, 8, 4096], P(None, 'col', 'blk'), may hold values from -6 to 6
- jacobian: float32 [5, 5], replicated, may hold values from -2.5 to 2.5
- areas: float32 [6, 4096], P(None, 'blk'), may hold values from 0.5 to 2
- volumes: float32 [4096], P('blk'), may hold values from 2 to 8
- neighbours: int32 [6, 4096], P(None, 'blk'), may hold values from -128 to 128, as said below
- block_cells: int32 [32], P('blk'), may hold values from 32 to 128, as said below
- bank: bfloat16 [128, 5, 4096], P('col', None, 'blk'), may hold values from -6 to 6
Outputs:
- hankel_pair: float32 [8, 8], P(None, 'col')
- hankel_bank: float32 [8, 128], P(None, 'col')
The draws below stay inside these ranges and needn't reach their ends.
Inputs may be any that keep to these rules, and one draw needn't show every extreme that they name: `neighbours`: each entry is 0 or an offset whose target cell lies inside the mesh; some entries are exactly 128 and -128. `block_cells`: every seventh block is full.
All inputs are finite; a program needn't handle non-finite values.
Results may differ from the reference program's by a relative error of at most 0.0003.
The reference program's roundings to bfloat16 on the way count: a program that leaves them out, or rounds other values in their place, can miss the bound.
Values may be sent and summed in bfloat16 or wider, within the bound.
A program may use at most 64 MiB of HBM per device.

```python
import math
import jax
import jax.numpy as jnp
from jax import lax

FIELDS = 5
NCOLS = 8
BANK = 128
REACH = 128
STEPS = 3
BCAP = 128
CELLS = 4096
BLOCKS = 32


def draw_neighbours(key, part):
    cell_ids = jnp.arange(CELLS, dtype=jnp.int32)
    key_near, key_middle, key_far, key_wall = jax.random.split(key, 4)
    near_step = jax.random.randint(key_near, (2, CELLS), 1, 5)
    middle_step = jax.random.randint(key_middle, (2, CELLS), 2, REACH // 4 + 1)
    far_step = jax.random.randint(key_far, (2, CELLS), REACH // 2, REACH + 1)
    marked = cell_ids % 61 == 0
    far_step = jnp.where(marked[None, :], REACH, far_step)
    offsets = jnp.stack([near_step[0], -near_step[1], middle_step[0], -middle_step[1], far_step[0], -far_step[1]])
    target = cell_ids[None, :] + offsets
    wall_face = jax.random.randint(key_wall, (6, CELLS), 0, 8) == 0
    wall_face = wall_face & jnp.logical_not(marked[None, :])
    inside = (target >= 0) & (target < CELLS)
    return jnp.where(wall_face | jnp.logical_not(inside), 0, offsets).astype(jnp.int32)


def draw_block_cells(key, part):
    counts = jax.random.randint(key, (BLOCKS,), BCAP // 4, BCAP + 1)
    block_ids = jnp.arange(BLOCKS, dtype=jnp.int32)
    return jnp.where(block_ids % 7 == 0, BCAP, counts).astype(jnp.int32)


def block_levels(stream_key, dims, cuts, smallest, largest):
    def one(position, parts):
        heights = jax.random.uniform(jax.random.fold_in(jax.random.fold_in(stream_key, 6), position), (parts,), jnp.float32, smallest / len(cuts), largest / len(cuts))
        return jnp.repeat(jnp.exp(heights), dims[position] // parts).reshape((-1,) + (1,) * (len(dims) - position - 1))

    gain = one(*cuts[0])
    for cut in cuts[1:]:
        gain = gain * one(*cut)
    return gain


def centred(own_key, extent, width, bound, cuts=(), kind=jnp.bfloat16):
    entries = width * jax.random.normal(own_key, extent, jnp.float32)
    if cuts:
        entries = entries * block_levels(own_key, extent, cuts, -0.22, 0.18)
    return jnp.clip(entries, -bound, bound).astype(kind)


def setup_inputs(seed: int = 0) -> dict:
    arg_keys = jax.random.split(jax.random.key(seed), 9)
    return {
        "direct_init": centred(arg_keys[0], (FIELDS, NCOLS, CELLS), 1.0, 6.0, ((1, 4), (2, 8)), jnp.float32),
        "adjoint_init": centred(arg_keys[1], (FIELDS, NCOLS, CELLS), 1.0, 6.0, ((1, 4), (2, 8)), jnp.float32),
        "jacobian": centred(arg_keys[2], (FIELDS, FIELDS), FIELDS ** -0.5, 2.5, (), jnp.float32),
        "areas": jnp.clip(jnp.exp(math.log(2.0) - 1.3862944 * jax.random.uniform(arg_keys[3], (6, CELLS), jnp.float32) ** block_levels(arg_keys[3], (6, CELLS), ((1, 8),), -0.2, 0.2)), 0.5, 2.0),
        "volumes": jnp.clip(jnp.exp(math.log(8.0) - 1.3862944 * jax.random.uniform(arg_keys[4], (CELLS,), jnp.float32) ** block_levels(arg_keys[4], (CELLS,), ((0, 8),), -0.2, 0.2)), 2.0, 8.0),
        "neighbours": draw_neighbours(jax.random.fold_in(arg_keys[8], 71), 0),
        "block_cells": draw_block_cells(jax.random.fold_in(arg_keys[8], 71), 0),
        "bank": centred(arg_keys[7], (BANK, FIELDS, CELLS), 1.0, 6.0, ((0, 4), (2, 8))),
    }


FACE_SIGNS = (1.0, -1.0, 1.0, -1.0, 1.0, -1.0)
time_step = 0.1


def face_rate(extended, index_map, face_coef, center, jacobian, split_at):
    flux_sum = jnp.zeros(center.shape, jnp.float32)
    drift_sum = jnp.zeros(center.shape, jnp.float32)
    for face_index in range(6):
        gathered = jnp.take(extended, index_map[face_index], axis=2)
        flux_sum = flux_sum + face_coef[face_index] * (gathered - center)
        drift_sum = drift_sum + (FACE_SIGNS[face_index] * face_coef[face_index]) * gathered
    forward = jnp.einsum('gh,hcm->gcm', jacobian, drift_sum[:, :split_at], precision=lax.Precision.HIGHEST)
    backward = jnp.einsum('hg,hcm->gcm', jacobian, drift_sum[:, split_at:], precision=lax.Precision.HIGHEST)
    return jnp.concatenate([flux_sum[:, :split_at] - forward, flux_sum[:, split_at:] + backward], axis=1)


def reference(direct_init, adjoint_init, jacobian, areas, volumes, neighbours, block_cells, bank):
    slot_ids = jnp.arange(CELLS, dtype=jnp.int32)
    live_limit = jnp.repeat(block_cells, BCAP)
    live_mask = (slot_ids % BCAP < live_limit).astype(jnp.float32)
    face_coef = live_mask[None, :] * areas / volumes[None, :]
    fields_now = jnp.concatenate([direct_init, adjoint_init], axis=1) * live_mask
    targets = jnp.clip(slot_ids[None, :] + neighbours, 0, CELLS - 1).astype(jnp.int32)
    index_map = jnp.where(neighbours == 0, CELLS, targets).astype(jnp.int32)
    zero_cell = jnp.zeros((FIELDS, 2 * NCOLS, 1), jnp.float32)

    def rate(values):
        return face_rate(jnp.concatenate([values, zero_cell], axis=2), index_map, face_coef, values, jacobian, NCOLS)

    for step_index in range(STEPS):
        first_rate = rate(fields_now)
        middle = fields_now + time_step * first_rate
        second_rate = rate(middle)
        fields_now = fields_now + (0.5 * time_step) * (first_rate + second_rate)
    cell_weight = volumes * live_mask * (FIELDS * CELLS) ** -0.5
    direct = (cell_weight * fields_now[:, :NCOLS]).astype(jnp.bfloat16)
    adjoint = fields_now[:, NCOLS:].astype(jnp.bfloat16)
    pair_sums = jnp.einsum('gam,gbm->ab', direct.astype(jnp.float32), adjoint.astype(jnp.float32), precision=lax.Precision.HIGHEST)
    flat_direct = direct.transpose(1, 0, 2).reshape(NCOLS, FIELDS * CELLS)
    flat_bank = bank.reshape(BANK, FIELDS * CELLS)
    projected = jnp.dot(flat_direct, flat_bank.T, preferred_element_type=jnp.float32)
    return pair_sums, projected
```

```python
import functools

import jax
import jax.numpy as jnp
from jax import lax
from jax.experimental import pallas as pl
from jax.experimental.pallas import tpu as pltpu
from jax.sharding import PartitionSpec as P

STEPS = 3
TIME_STEP = 0.1
LANES = 128
ROWS = 32
SLOTS = 8
MESH = pl.DeviceIdType.MESH


def lane_take(values, index):
    return jnp.take_along_axis(values, index, axis=1, mode="promise_in_bounds")


def kernel(
    n_blk, n_col, scale_norm,
    jac, cells, direct, adjoint, areas, volumes, neighbours, bank,
    out,
    ext, state, middle, rates, coef, index, side, coef_sum, mixing, bank_rows, rhs, adj_rows, messages, parts,
    halo_send, halo_recv, col_send, col_recv, sum_send, sum_recv,
):
    fields = direct.shape[0]
    tiles = direct.shape[2] // LANES
    me = lax.axis_index("blk")
    mine = lax.axis_index("col")

    barrier = pltpu.get_barrier_semaphore()

    def greet(axis, own, count):
        def one(step, carry):
            peer = lax.rem(own + step, count)
            pl.semaphore_signal(barrier, inc=1, device_id={axis: peer}, device_id_type=MESH)
            return carry
        lax.fori_loop(1, count, one, 0, unroll=count <= 16)

    greet("blk", me, n_blk)
    greet("col", mine, n_col)

    lane = lax.broadcasted_iota(jnp.int32, (1, LANES), 1)
    for t in range(tiles):
        part = pl.ds(t * LANES, LANES)
        live = jnp.where(lane < cells[t], 1.0, 0.0)
        for g in range(fields):
            ext[6 + t, 4 * g:4 * g + 2, :] = direct[g, :, part] * live
            ext[6 + t, 4 * g + 2:4 * g + 4, :] = adjoint[g, :, part] * live
        ext[6 + t, 20:26, :] = live * areas[:, part] / volumes[:, part]
        ext[6 + t, 26:32, :] = neighbours[:, part].astype(jnp.float32)

    pl.semaphore_wait(barrier, n_blk - 1 + n_col - 1)

    hops = (
        (1, (6, 4), (2, 4)),
        (-1, (6, 4), (10, 4)),
        (2, (8, 2), (0, 2)),
        (-2, (6, 2), (14, 2)),
    )

    def halo(k, peer):
        distance, source, target = hops[k]
        return pltpu.make_async_remote_copy(
            src_ref=ext.at[pl.ds(*source)],
            dst_ref=ext.at[pl.ds(*target)],
            send_sem=halo_send.at[k],
            recv_sem=halo_recv.at[k],
            device_id={"blk": peer},
            device_id_type=MESH,
        )

    for k, (distance, source, target) in enumerate(hops):
        goes = (me + distance < n_blk) if distance > 0 else (me + distance >= 0)

        @pl.when(goes)
        def _():
            halo(k, me + distance).start()

        comes = (me - distance >= 0) if distance > 0 else (me - distance < n_blk)

        @pl.when(jnp.logical_not(comes))
        def _():
            ext[pl.ds(*target)] = jnp.zeros((target[1], ROWS, LANES), jnp.float32)

    sub = lax.broadcasted_iota(jnp.int32, (8, LANES), 0)
    is_direct = lax.rem(sub, 4) < 2
    for g in range(fields):
        for h in range(fields):
            mixing[g * fields + h] = jnp.where(is_direct, -jac[g, h], jac[h, g])
    bank_rows[:, 0:fields, :] = bank[...].astype(jnp.float32)
    span = tiles * LANES
    count = bank.shape[0]
    for g in range(fields):
        rhs[0:count, g * span:(g + 1) * span] = bank_rows[:, g, :].astype(jnp.bfloat16)
    adj_rows[...] = jnp.zeros(adj_rows.shape, jnp.float32)

    for k, (distance, source, target) in enumerate(hops):
        comes = (me - distance >= 0) if distance > 0 else (me - distance < n_blk)

        @pl.when(comes)
        def _():
            halo(k, me).wait_recv()

    low = sub < 4

    def both(p, row):
        a = jnp.broadcast_to(ext[p, row:row + 1, :], (8, LANES))
        b = jnp.broadcast_to(ext[15 - p, row:row + 1, :], (8, LANES))
        return jnp.where(low, a, b)

    wide = lax.broadcasted_iota(jnp.int32, (8, LANES), 1)
    for p in range(SLOTS):
        for g in range(fields):
            state[p, g] = jnp.concatenate(
                [ext[p, 4 * g:4 * g + 4, :], ext[15 - p, 4 * g:4 * g + 4, :]], axis=0
            )
        if p == 0:
            continue
        total = jnp.zeros((8, LANES), jnp.float32)
        for f in range(6):
            offset = both(p, 26 + f).astype(jnp.int32)
            c = both(p, 20 + f)
            total = total + c
            coef[p, f] = jnp.where(offset == 0, 0.0, c)
            target = wide + offset
            index[p, f] = jnp.bitwise_and(target, LANES - 1)
            way = jnp.where(target < 0, -1, jnp.where(target >= LANES, 1, 0))
            side[p, f] = jnp.where(low, way, -way)
        coef_sum[p] = total

    def swap_middle(buffer):
        for g in range(fields):
            buffer[SLOTS, g] = pltpu.roll(buffer[SLOTS - 1, g], 4, 0)

    def rate(buffer, p):
        even = [jnp.zeros((8, LANES), jnp.float32) for _ in range(fields)]
        odd = [jnp.zeros((8, LANES), jnp.float32) for _ in range(fields)]
        center = [buffer[p, g] for g in range(fields)]
        for f in range(6):
            ix = index[p, f]
            sd = side[p, f]
            c = coef[p, f]
            outer = sd < 0
            inner = sd > 0
            for g in range(fields):
                got = lane_take(center[g], ix)
                got = jnp.where(outer, lane_take(buffer[p - 1, g], ix), got)
                got = jnp.where(inner, lane_take(buffer[p + 1, g], ix), got)
                if f % 2 == 0:
                    even[g] = even[g] + c * got
                else:
                    odd[g] = odd[g] + c * got
        drift = [even[g] - odd[g] for g in range(fields)]
        result = []
        for g in range(fields):
            value = even[g] + odd[g] - coef_sum[p] * center[g]
            for h in range(fields):
                value = value + mixing[g * fields + h] * drift[h]
            result.append(value)
        return center, result

    for step in range(STEPS):
        swap_middle(state)

        def first(p, carry):
            center, value = rate(state, p)
            for g in range(fields):
                rates[p, g] = value[g]
                middle[p, g] = center[g] + TIME_STEP * value[g]
            return carry

        lax.fori_loop(2 * step + 1, SLOTS, first, 0, unroll=UNROLL)
        swap_middle(middle)

        def second(p, carry):
            _, value = rate(middle, p)
            for g in range(fields):
                state[p, g] = state[p, g] + (0.5 * TIME_STEP) * (rates[p, g] + value[g])
            return carry

        lax.fori_loop(2 * step + 2, SLOTS, second, 0, unroll=UNROLL)

    direct_rows = []
    for g in range(fields):
        for t in range(tiles):
            e = 6 + t
            p, row = (e, 0) if e < SLOTS else (15 - e, 4)
            live = jnp.where(lane < cells[t], 1.0, 0.0)
            weight = volumes[:, t * LANES:(t + 1) * LANES] * live * scale_norm
            column = pl.ds(g * span + t * LANES, LANES)
            direct_rows.append(weight * state[p, g, row:row + 2, :])
            adj_rows[0:2, column] = state[p, g, row + 2:row + 4, :]
    messages[mine] = jnp.concatenate(direct_rows, axis=1).astype(jnp.bfloat16)

    def column_copy(step, slot, peer):
        return pltpu.make_async_remote_copy(
            src_ref=messages.at[slot],
            dst_ref=messages.at[slot],
            send_sem=col_send.at[step],
            recv_sem=col_recv.at[slot],
            device_id={"col": peer},
            device_id_type=MESH,
        )

    for step in range(1, n_col):
        column_copy(step, mine, lax.rem(mine + step, n_col)).start()
    rhs[count:count + 16, :] = adj_rows[...].astype(jnp.bfloat16)
    for step in range(1, n_col):
        slot = lax.rem(mine + step, n_col)
        column_copy(step, slot, slot).wait_recv()

    lhs = jnp.concatenate(
        [messages[c].astype(jnp.float32) for c in range(n_col)], axis=0
    ).astype(jnp.bfloat16)
    product = lax.dot_general(
        lhs, rhs[...], (((1,), (1,)), ((), ())), preferred_element_type=jnp.float32
    )
    parts[me] = product

    def sum_copy(step, slot, peer):
        return pltpu.make_async_remote_copy(
            src_ref=parts.at[slot],
            dst_ref=parts.at[slot],
            send_sem=sum_send.at[step],
            recv_sem=sum_recv.at[slot],
            device_id={"blk": peer},
            device_id_type=MESH,
        )

    def start_sum(step, carry):
        sum_copy(step, me, lax.rem(me + step, n_blk)).start()
        return carry

    def wait_sum(step, carry):
        slot = lax.rem(me + step, n_blk)
        sum_copy(step, slot, slot).wait_recv()
        return carry

    def wait_sent(step, carry):
        sum_copy(step, me, lax.rem(me + step, n_blk)).wait_send()
        return carry

    few = n_blk <= 16
    lax.fori_loop(1, n_blk, start_sum, 0, unroll=few)
    lax.fori_loop(1, n_blk, wait_sum, 0, unroll=few)
    out[...] = lax.fori_loop(
        0, n_blk, lambda i, total: total + parts[i], jnp.zeros(out.shape, jnp.float32), unroll=few
    )

    for k, (distance, source, target) in enumerate(hops):
        goes = (me + distance < n_blk) if distance > 0 else (me + distance >= 0)

        @pl.when(goes)
        def _():
            halo(k, me).wait_send()

    for step in range(1, n_col):
        column_copy(step, mine, mine).wait_send()
    lax.fori_loop(1, n_blk, wait_sent, 0, unroll=few)


UNROLL = True


def local(n_blk, n_col, direct_init, adjoint_init, jacobian, areas, volumes, neighbours, block_cells, bank):
    fields, own, cell_count = direct_init.shape
    count = bank.shape[0]
    wide = fields * cell_count
    scale_norm = (fields * cell_count * n_blk) ** (-0.5)
    vmem = pl.BlockSpec(memory_space=pltpu.VMEM)
    smem = pl.BlockSpec(memory_space=pltpu.SMEM)
    f32 = jnp.float32
    dma = pltpu.SemaphoreType.DMA
    total = pl.pallas_call(
        functools.partial(kernel, n_blk, n_col, scale_norm),
        out_shape=jax.ShapeDtypeStruct((n_col * own, count + 16), f32),
        in_specs=[smem, smem] + [vmem] * 6,
        out_specs=vmem,
        scratch_shapes=[
            pltpu.VMEM((16, ROWS, LANES), f32),
            pltpu.VMEM((SLOTS + 1, fields, 8, LANES), f32),
            pltpu.VMEM((SLOTS + 1, fields, 8, LANES), f32),
            pltpu.VMEM((SLOTS, fields, 8, LANES), f32),
            pltpu.VMEM((SLOTS, 6, 8, LANES), f32),
            pltpu.VMEM((SLOTS, 6, 8, LANES), jnp.int32),
            pltpu.VMEM((SLOTS, 6, 8, LANES), jnp.int32),
            pltpu.VMEM((SLOTS, 8, LANES), f32),
            pltpu.VMEM((fields * fields, 8, LANES), f32),
            pltpu.VMEM((count, 8, cell_count), f32),
            pltpu.VMEM((count + 16, wide), jnp.bfloat16),
            pltpu.VMEM((16, wide), f32),
            pltpu.VMEM((n_col, own, wide), jnp.bfloat16),
            pltpu.VMEM((n_blk, n_col * own, count + 16), f32),
            dma((4,)), dma((4,)), dma((n_col,)), dma((n_col,)), dma((n_blk,)), dma((n_blk,)),
        ],
        compiler_params=pltpu.CompilerParams(collective_id=0, has_side_effects=True),
        name="hankel",
    )(jacobian, block_cells, direct_init, adjoint_init, areas, volumes.reshape(1, cell_count), neighbours, bank)
    return total[:, count:count + own], total[:, :count]


def solution(mesh):
    return jax.shard_map(
        functools.partial(local, mesh.shape["blk"], mesh.shape["col"]),
        mesh=mesh,
        in_specs=(
            P(None, "col", "blk"),
            P(None, "col", "blk"),
            P(),
            P(None, "blk"),
            P("blk"),
            P(None, "blk"),
            P("blk"),
            P("col", None, "blk"),
        ),
        out_specs=(P(None, "col"), P(None, "col")),
        check_vma=False,
    )
```

```python
import functools

import jax
import jax.numpy as jnp
from jax import lax
from jax.experimental import pallas as pl
from jax.experimental.pallas import tpu as pltpu
from jax.sharding import PartitionSpec as P

STEPS = 3
TIME_STEP = 0.1
LANES = 128
ROWS = 32
SLOTS = 8
MESH = pl.DeviceIdType.MESH


def lane_take(values, index):
    return jnp.take_along_axis(values, index, axis=1, mode="promise_in_bounds")


def kernel(
    n_blk, n_col, scale_norm,
    jac_in, cells_in, direct_in, adjoint_in, areas_in, volumes_in, neighbours_in, bank_in,
    out_pair, out_bank,
    ext, state, middle, rates, coef, index, side, coef_sum, mixing, adj_rows, messages, parts,
    jac, cells, direct, adjoint, areas, volumes, neighbours, bank, loaded,
    halo_send, halo_recv, col_send, col_recv, sum_send, sum_recv,
):
    fields = direct.shape[0]
    tiles = direct.shape[2] // LANES
    me = lax.axis_index("blk")
    mine = lax.axis_index("col")

    loads = [
        pltpu.make_async_copy(source, target, loaded.at[k])
        for k, (source, target) in enumerate((
            (cells_in, cells), (direct_in, direct), (adjoint_in, adjoint), (areas_in, areas),
            (volumes_in, volumes), (neighbours_in, neighbours), (jac_in, jac), (bank_in, bank),
        ))
    ]
    for load in loads[:6]:
        load.start()

    barrier = pltpu.get_barrier_semaphore()

    def greet(axis, own, count):
        def one(step, carry):
            peer = lax.rem(own + step, count)
            pl.semaphore_signal(barrier, inc=1, device_id={axis: peer}, device_id_type=MESH)
            return carry
        lax.fori_loop(1, count, one, 0, unroll=count <= 16)

    greet("blk", me, n_blk)
    greet("col", mine, n_col)
    for load in loads[6:]:
        load.start()
    for load in loads[:6]:
        load.wait()

    lane = lax.broadcasted_iota(jnp.int32, (1, LANES), 1)
    for t in range(tiles):
        part = pl.ds(t * LANES, LANES)
        live = jnp.where(lane < cells[t], 1.0, 0.0)
        for g in range(fields):
            ext[6 + t, 4 * g:4 * g + 2, :] = direct[g, :, part] * live
            ext[6 + t, 4 * g + 2:4 * g + 4, :] = adjoint[g, :, part] * live
        ext[6 + t, 20:26, :] = live * areas[:, part] / volumes[:, part]
        ext[6 + t, 26:32, :] = neighbours[:, part].astype(jnp.float32)

    pl.semaphore_wait(barrier, n_blk - 1 + n_col - 1)

    hops = (
        (1, (6, 4), (2, 4)),
        (-1, (6, 4), (10, 4)),
        (2, (8, 2), (0, 2)),
        (-2, (6, 2), (14, 2)),
    )

    def halo(k, peer):
        distance, source, target = hops[k]
        return pltpu.make_async_remote_copy(
            src_ref=ext.at[pl.ds(*source)],
            dst_ref=ext.at[pl.ds(*target)],
            send_sem=halo_send.at[k],
            recv_sem=halo_recv.at[k],
            device_id={"blk": peer},
            device_id_type=MESH,
        )

    for k, (distance, source, target) in enumerate(hops):
        goes = (me + distance < n_blk) if distance > 0 else (me + distance >= 0)

        @pl.when(goes)
        def _():
            halo(k, me + distance).start()

        comes = (me - distance >= 0) if distance > 0 else (me - distance < n_blk)

        @pl.when(jnp.logical_not(comes))
        def _():
            ext[pl.ds(*target)] = jnp.zeros((target[1], ROWS, LANES), jnp.float32)

    for load in loads[6:]:
        load.wait()
    sub = lax.broadcasted_iota(jnp.int32, (8, LANES), 0)
    is_direct = lax.rem(sub, 4) < 2
    for g in range(fields):
        for h in range(fields):
            mixing[g * fields + h] = jnp.where(is_direct, -jac[g, h], jac[h, g])
    span = tiles * LANES
    count = bank.shape[1]
    adj_rows[...] = jnp.zeros(adj_rows.shape, jnp.float32)

    for k, (distance, source, target) in enumerate(hops):
        comes = (me - distance >= 0) if distance > 0 else (me - distance < n_blk)

        @pl.when(comes)
        def _():
            halo(k, me).wait_recv()

    low = sub < 4

    def both(p, row):
        a = jnp.broadcast_to(ext[p, row:row + 1, :], (8, LANES))
        b = jnp.broadcast_to(ext[15 - p, row:row + 1, :], (8, LANES))
        return jnp.where(low, a, b)

    wide = lax.broadcasted_iota(jnp.int32, (8, LANES), 1)
    for p in range(SLOTS):
        for g in range(fields):
            state[p, g] = jnp.concatenate(
                [ext[p, 4 * g:4 * g + 4, :], ext[15 - p, 4 * g:4 * g + 4, :]], axis=0
            )
        if p == 0:
            continue
        total = jnp.zeros((8, LANES), jnp.float32)
        for f in range(6):
            offset = both(p, 26 + f).astype(jnp.int32)
            c = both(p, 20 + f)
            total = total + c
            coef[p, f] = jnp.where(offset == 0, 0.0, c)
            target = wide + offset
            index[p, f] = jnp.bitwise_and(target, LANES - 1)
            way = jnp.where(target < 0, -1, jnp.where(target >= LANES, 1, 0))
            side[p, f] = jnp.where(low, way, -way)
        coef_sum[p] = total

    def swap_middle(buffer):
        for g in range(fields):
            buffer[SLOTS, g] = pltpu.roll(buffer[SLOTS - 1, g], 4, 0)

    def rate(buffer, p):
        even = [jnp.zeros((8, LANES), jnp.float32) for _ in range(fields)]
        odd = [jnp.zeros((8, LANES), jnp.float32) for _ in range(fields)]
        center = [buffer[p, g] for g in range(fields)]
        for f in range(6):
            ix = index[p, f]
            sd = side[p, f]
            c = coef[p, f]
            outer = sd < 0
            inner = sd > 0
            for g in range(fields):
                got = lane_take(center[g], ix)
                got = jnp.where(outer, lane_take(buffer[p - 1, g], ix), got)
                got = jnp.where(inner, lane_take(buffer[p + 1, g], ix), got)
                if f % 2 == 0:
                    even[g] = even[g] + c * got
                else:
                    odd[g] = odd[g] + c * got
        drift = [even[g] - odd[g] for g in range(fields)]
        result = []
        for g in range(fields):
            value = even[g] + odd[g] - coef_sum[p] * center[g]
            for h in range(fields):
                value = value + mixing[g * fields + h] * drift[h]
            result.append(value)
        return center, result

    for step in range(STEPS):
        swap_middle(state)

        def first(p, carry):
            center, value = rate(state, p)
            for g in range(fields):
                rates[p, g] = value[g]
                middle[p, g] = center[g] + TIME_STEP * value[g]
            return carry

        lax.fori_loop(2 * step + 1, SLOTS, first, 0, unroll=UNROLL)
        swap_middle(middle)

        def second(p, carry):
            _, value = rate(middle, p)
            for g in range(fields):
                state[p, g] = state[p, g] + (0.5 * TIME_STEP) * (rates[p, g] + value[g])
            return carry

        lax.fori_loop(2 * step + 2, SLOTS, second, 0, unroll=UNROLL)

    direct_rows = []
    for g in range(fields):
        for t in range(tiles):
            e = 6 + t
            p, row = (e, 0) if e < SLOTS else (15 - e, 4)
            live = jnp.where(lane < cells[t], 1.0, 0.0)
            weight = volumes[:, t * LANES:(t + 1) * LANES] * live * scale_norm
            column = pl.ds(g * span + t * LANES, LANES)
            direct_rows.append(weight * state[p, g, row:row + 2, :])
            adj_rows[0:2, column] = state[p, g, row + 2:row + 4, :]
    messages[mine] = jnp.concatenate(direct_rows, axis=1).astype(jnp.bfloat16)

    def column_copy(step, slot, peer):
        return pltpu.make_async_remote_copy(
            src_ref=messages.at[slot],
            dst_ref=messages.at[slot],
            send_sem=col_send.at[step],
            recv_sem=col_recv.at[slot],
            device_id={"col": peer},
            device_id_type=MESH,
        )

    for step in range(1, n_col):
        column_copy(step, mine, lax.rem(mine + step, n_col)).start()
    own_adjoint = adj_rows[...].astype(jnp.bfloat16)
    for step in range(1, n_col):
        slot = lax.rem(mine + step, n_col)
        column_copy(step, slot, slot).wait_recv()

    lhs = jnp.concatenate(
        [messages[c].astype(jnp.float32) for c in range(n_col)], axis=0
    ).astype(jnp.bfloat16)
    contract = (((1,), (1,)), ((), ()))
    bank_part = jnp.zeros((lhs.shape[0], count), jnp.float32)
    for g in range(fields):
        bank_part = bank_part + lax.dot_general(
            lhs[:, g * span:(g + 1) * span], bank[g], contract, preferred_element_type=jnp.float32
        )
    pair_part = lax.dot_general(own_adjoint, lhs, contract, preferred_element_type=jnp.float32)
    parts[me] = jnp.concatenate([bank_part, pair_part[0:8]], axis=1)

    def sum_copy(step, slot, peer):
        return pltpu.make_async_remote_copy(
            src_ref=parts.at[slot],
            dst_ref=parts.at[slot],
            send_sem=sum_send.at[step],
            recv_sem=sum_recv.at[slot],
            device_id={"blk": peer},
            device_id_type=MESH,
        )

    def start_sum(step, carry):
        sum_copy(step, me, lax.rem(me + step, n_blk)).start()
        return carry

    def wait_sum(step, carry):
        slot = lax.rem(me + step, n_blk)
        sum_copy(step, slot, slot).wait_recv()
        return carry

    def wait_sent(step, carry):
        sum_copy(step, me, lax.rem(me + step, n_blk)).wait_send()
        return carry

    few = n_blk <= 16
    lax.fori_loop(1, n_blk, start_sum, 0, unroll=few)
    lax.fori_loop(1, n_blk, wait_sum, 0, unroll=few)
    total = lax.fori_loop(
        0, n_blk, lambda i, total: total + parts[i], jnp.zeros(parts.shape[1:], jnp.float32), unroll=few
    )
    out_bank[...] = total[:, 0:count]
    out_pair[...] = total[0:out_pair.shape[0], count:count + lhs.shape[0]]

    for k, (distance, source, target) in enumerate(hops):
        goes = (me + distance < n_blk) if distance > 0 else (me + distance >= 0)

        @pl.when(goes)
        def _():
            halo(k, me).wait_send()

    for step in range(1, n_col):
        column_copy(step, mine, mine).wait_send()
    lax.fori_loop(1, n_blk, wait_sent, 0, unroll=few)


UNROLL = True


def finish(pair_in, bank_in, pair_out, bank_out):
    pair_out[...] = pair_in[...]
    bank_out[...] = bank_in[...]


def local(n_blk, n_col, direct_init, adjoint_init, jacobian, areas, volumes, neighbours, block_cells, bank):
    fields, own, cell_count = direct_init.shape
    count = bank.shape[0]
    wide = fields * cell_count
    scale_norm = (fields * cell_count * n_blk) ** (-0.5)
    vmem = pl.BlockSpec(memory_space=pltpu.VMEM)
    f32 = jnp.float32
    dma = pltpu.SemaphoreType.DMA
    pair, projected = pl.pallas_call(
        functools.partial(kernel, n_blk, n_col, scale_norm),
        out_shape=(
            jax.ShapeDtypeStruct((own, n_col * own), f32),
            jax.ShapeDtypeStruct((n_col * own, count), f32),
        ),
        in_specs=[pl.BlockSpec(memory_space=pl.ANY)] * 8,
        out_specs=(vmem, vmem),
        scratch_shapes=[
            pltpu.VMEM((16, ROWS, LANES), f32),
            pltpu.VMEM((SLOTS + 1, fields, 8, LANES), f32),
            pltpu.VMEM((SLOTS + 1, fields, 8, LANES), f32),
            pltpu.VMEM((SLOTS, fields, 8, LANES), f32),
            pltpu.VMEM((SLOTS, 6, 8, LANES), f32),
            pltpu.VMEM((SLOTS, 6, 8, LANES), jnp.int32),
            pltpu.VMEM((SLOTS, 6, 8, LANES), jnp.int32),
            pltpu.VMEM((SLOTS, 8, LANES), f32),
            pltpu.VMEM((fields * fields, 8, LANES), f32),
            pltpu.VMEM((16, wide), f32),
            pltpu.VMEM((n_col, own, wide), jnp.bfloat16),
            pltpu.VMEM((n_blk, n_col * own, count + n_col * own), f32),
            pltpu.SMEM(jacobian.shape, f32),
            pltpu.SMEM(block_cells.shape, jnp.int32),
            pltpu.VMEM(direct_init.shape, f32),
            pltpu.VMEM(adjoint_init.shape, f32),
            pltpu.VMEM(areas.shape, f32),
            pltpu.VMEM((1, cell_count), f32),
            pltpu.VMEM(neighbours.shape, jnp.int32),
            pltpu.VMEM((fields, count, cell_count), jnp.bfloat16),
            dma((8,)),
            dma((4,)), dma((4,)), dma((n_col,)), dma((n_col,)), dma((n_blk,)), dma((n_blk,)),
        ],
        compiler_params=pltpu.CompilerParams(collective_id=0, has_side_effects=True),
        name="hankel",
    )(jacobian, block_cells, direct_init, adjoint_init, areas, volumes.reshape(1, cell_count), neighbours, bank.transpose(1, 0, 2))
    pair, projected = pl.pallas_call(
        finish,
        out_shape=(
            jax.ShapeDtypeStruct((own, n_col * own), f32),
            jax.ShapeDtypeStruct((n_col * own, count), f32),
        ),
        in_specs=[vmem, vmem],
        out_specs=(vmem, vmem),
        name="finish",
    )(pair, projected)
    return pair.T, projected


def solution(mesh):
    return jax.shard_map(
        functools.partial(local, mesh.shape["blk"], mesh.shape["col"]),
        mesh=mesh,
        in_specs=(
            P(None, "col", "blk"),
            P(None, "col", "blk"),
            P(),
            P(None, "blk"),
            P("blk"),
            P(None, "blk"),
            P("blk"),
            P("col", None, "blk"),
        ),
        out_specs=(P(None, "col"), P(None, "col")),
        check_vma=False,
    )
```

```python
import functools

import jax
import jax.numpy as jnp
from jax import lax
from jax.experimental import pallas as pl
from jax.experimental.pallas import tpu as pltpu
from jax.sharding import PartitionSpec as P

STEPS = 3
TIME_STEP = 0.1
LANES = 128
ROWS = 32
SLOTS = 8
MESH = pl.DeviceIdType.MESH


def lane_take(values, index):
    return jnp.take_along_axis(values, index, axis=1, mode="promise_in_bounds")


def kernel(
    n_blk, n_col, scale_norm,
    jac_in, cells_in, direct_in, adjoint_in, areas_in, volumes_in, neighbours_in, bank_in,
    out_pair, out_bank,
    ext, state, middle, rates, coef, index, side, coef_sum, mixing, adj_rows, messages, parts,
    jac, cells, direct, adjoint, areas, volumes, neighbours, bank, loaded,
    halo_send, halo_recv, col_send, col_recv, sum_send, sum_recv,
):
    fields = direct.shape[0]
    tiles = direct.shape[2] // LANES
    me = lax.axis_index("blk")
    mine = lax.axis_index("col")

    loads = [
        pltpu.make_async_copy(source, target, loaded.at[k])
        for k, (source, target) in enumerate((
            (cells_in, cells), (direct_in, direct), (adjoint_in, adjoint), (areas_in, areas),
            (volumes_in, volumes), (neighbours_in, neighbours), (jac_in, jac), (bank_in, bank),
        ))
    ]
    for load in loads[:6]:
        load.start()

    barrier = pltpu.get_barrier_semaphore()

    def greet(axis, own, count):
        def one(step, carry):
            peer = lax.rem(own + step, count)
            pl.semaphore_signal(barrier, inc=1, device_id={axis: peer}, device_id_type=MESH)
            return carry
        lax.fori_loop(1, count, one, 0, unroll=count <= 16)

    greet("blk", me, n_blk)
    greet("col", mine, n_col)
    for load in loads[6:]:
        load.start()
    for load in loads[:6]:
        load.wait()

    lane = lax.broadcasted_iota(jnp.int32, (1, LANES), 1)
    for t in range(tiles):
        part = pl.ds(t * LANES, LANES)
        live = jnp.where(lane < cells[t], 1.0, 0.0)
        for g in range(fields):
            ext[6 + t, 4 * g:4 * g + 2, :] = direct[g, :, part] * live
            ext[6 + t, 4 * g + 2:4 * g + 4, :] = adjoint[g, :, part] * live
        ext[6 + t, 20:26, :] = live * areas[:, part] / volumes[:, part]
        ext[6 + t, 26:32, :] = neighbours[:, part].astype(jnp.float32)

    pl.semaphore_wait(barrier, n_blk - 1 + n_col - 1)

    hops = (
        (1, (8, 2), (4, 2)),
        (-1, (6, 2), (10, 2)),
        (1, (6, 2), (2, 2)),
        (-1, (8, 2), (12, 2)),
        (2, (8, 2), (0, 2)),
        (-2, (6, 2), (14, 2)),
    )

    def halo(k, peer):
        distance, source, target = hops[k]
        return pltpu.make_async_remote_copy(
            src_ref=ext.at[pl.ds(*source)],
            dst_ref=ext.at[pl.ds(*target)],
            send_sem=halo_send.at[k],
            recv_sem=halo_recv.at[k],
            device_id={"blk": peer},
            device_id_type=MESH,
        )

    for k, (distance, source, target) in enumerate(hops):
        goes = (me + distance < n_blk) if distance > 0 else (me + distance >= 0)

        @pl.when(goes)
        def _():
            halo(k, me + distance).start()

        comes = (me - distance >= 0) if distance > 0 else (me - distance < n_blk)

        @pl.when(jnp.logical_not(comes))
        def _():
            ext[pl.ds(*target)] = jnp.zeros((target[1], ROWS, LANES), jnp.float32)

    for load in loads[6:]:
        load.wait()
    sub = lax.broadcasted_iota(jnp.int32, (8, LANES), 0)
    is_direct = lax.rem(sub, 4) < 2
    for g in range(fields):
        for h in range(fields):
            mixing[g * fields + h] = jnp.where(is_direct, -jac[g, h], jac[h, g])
    span = tiles * LANES
    count = bank.shape[1]
    adj_rows[...] = jnp.zeros(adj_rows.shape, jnp.float32)

    def arrive(ids):
        for k in ids:
            distance = hops[k][0]
            comes = (me - distance >= 0) if distance > 0 else (me - distance < n_blk)

            @pl.when(comes)
            def _():
                halo(k, me).wait_recv()

    low = sub < 4

    def both(p, row):
        a = jnp.broadcast_to(ext[p, row:row + 1, :], (8, LANES))
        b = jnp.broadcast_to(ext[15 - p, row:row + 1, :], (8, LANES))
        return jnp.where(low, a, b)

    wide = lax.broadcasted_iota(jnp.int32, (8, LANES), 1)

    def unpack(p):
        for g in range(fields):
            state[p, g] = jnp.concatenate(
                [ext[p, 4 * g:4 * g + 4, :], ext[15 - p, 4 * g:4 * g + 4, :]], axis=0
            )
        if p == 0:
            return
        total = jnp.zeros((8, LANES), jnp.float32)
        for f in range(6):
            offset = both(p, 26 + f).astype(jnp.int32)
            c = both(p, 20 + f)
            total = total + c
            coef[p, f] = jnp.where(offset == 0, 0.0, c)
            target = wide + offset
            index[p, f] = jnp.bitwise_and(target, LANES - 1)
            way = jnp.where(target < 0, -1, jnp.where(target >= LANES, 1, 0))
            side[p, f] = jnp.where(low, way, -way)
        coef_sum[p] = total

    def swap_middle(buffer):
        for g in range(fields):
            buffer[SLOTS, g] = pltpu.roll(buffer[SLOTS - 1, g], 4, 0)

    def rate(buffer, p):
        even = [jnp.zeros((8, LANES), jnp.float32) for _ in range(fields)]
        odd = [jnp.zeros((8, LANES), jnp.float32) for _ in range(fields)]
        center = [buffer[p, g] for g in range(fields)]
        for f in range(6):
            ix = index[p, f]
            sd = side[p, f]
            c = coef[p, f]
            outer = sd < 0
            inner = sd > 0
            for g in range(fields):
                got = lane_take(center[g], ix)
                got = jnp.where(outer, lane_take(buffer[p - 1, g], ix), got)
                got = jnp.where(inner, lane_take(buffer[p + 1, g], ix), got)
                if f % 2 == 0:
                    even[g] = even[g] + c * got
                else:
                    odd[g] = odd[g] + c * got
        drift = [even[g] - odd[g] for g in range(fields)]
        result = []
        for g in range(fields):
            value = even[g] + odd[g] - coef_sum[p] * center[g]
            for h in range(fields):
                value = value + mixing[g * fields + h] * drift[h]
            result.append(value)
        return center, result

    def advance(stage, p):
        if stage % 2:
            center, value = rate(state, p)
            for g in range(fields):
                rates[p, g] = value[g]
                middle[p, g] = center[g] + TIME_STEP * value[g]
        else:
            _, value = rate(middle, p)
            for g in range(fields):
                state[p, g] = state[p, g] + (0.5 * TIME_STEP) * (rates[p, g] + value[g])
        if p == SLOTS - 1 and stage < 2 * STEPS:
            swap_middle(middle if stage % 2 else state)

    weights = []
    for t in range(tiles):
        live = jnp.where(lane < cells[t], 1.0, 0.0)
        weights.append(volumes[:, t * LANES:(t + 1) * LANES] * live * scale_norm)
    lowest, done = SLOTS, {stage: SLOTS for stage in range(1, 2 * STEPS + 1)}
    for bottom, ids in ((6, ()), (4, (0, 1)), (0, (2, 3, 4, 5))):
        arrive(ids)
        for p in range(lowest - 1, bottom - 1, -1):
            unpack(p)
        if lowest == SLOTS:
            swap_middle(state)
        lowest = bottom
        for stage in range(1, 2 * STEPS + 1):
            start = min(bottom + stage, SLOTS)
            for p in range(start, done[stage]):
                advance(stage, p)
            done[stage] = start

    direct_rows = []
    for g in range(fields):
        for t in range(tiles):
            e = 6 + t
            p, row = (e, 0) if e < SLOTS else (15 - e, 4)
            column = pl.ds(g * span + t * LANES, LANES)
            direct_rows.append(weights[t] * state[p, g, row:row + 2, :])
            adj_rows[0:2, column] = state[p, g, row + 2:row + 4, :]
    messages[mine] = jnp.concatenate(direct_rows, axis=1).astype(jnp.bfloat16)

    def column_copy(step, slot, peer):
        return pltpu.make_async_remote_copy(
            src_ref=messages.at[slot],
            dst_ref=messages.at[slot],
            send_sem=col_send.at[step],
            recv_sem=col_recv.at[slot],
            device_id={"col": peer},
            device_id_type=MESH,
        )

    for step in range(1, n_col):
        column_copy(step, mine, lax.rem(mine + step, n_col)).start()
    own_adjoint = adj_rows[...].astype(jnp.bfloat16)
    for step in range(1, n_col):
        slot = lax.rem(mine + step, n_col)
        column_copy(step, slot, slot).wait_recv()

    lhs = jnp.concatenate(
        [messages[c].astype(jnp.float32) for c in range(n_col)], axis=0
    ).astype(jnp.bfloat16)
    contract = (((1,), (1,)), ((), ()))
    bank_part = jnp.zeros((lhs.shape[0], count), jnp.float32)
    for g in range(fields):
        bank_part = bank_part + lax.dot_general(
            lhs[:, g * span:(g + 1) * span], bank[g], contract, preferred_element_type=jnp.float32
        )
    pair_part = lax.dot_general(own_adjoint, lhs, contract, preferred_element_type=jnp.float32)
    parts[me] = jnp.concatenate([bank_part, pair_part[0:8]], axis=1)

    def sum_copy(step, slot, peer):
        return pltpu.make_async_remote_copy(
            src_ref=parts.at[slot],
            dst_ref=parts.at[slot],
            send_sem=sum_send.at[step],
            recv_sem=sum_recv.at[slot],
            device_id={"blk": peer},
            device_id_type=MESH,
        )

    def start_sum(step, carry):
        sum_copy(step, me, lax.rem(me + step, n_blk)).start()
        return carry

    def wait_sum(step, carry):
        slot = lax.rem(me + step, n_blk)
        sum_copy(step, slot, slot).wait_recv()
        return carry

    def wait_sent(step, carry):
        sum_copy(step, me, lax.rem(me + step, n_blk)).wait_send()
        return carry

    few = n_blk <= 16
    lax.fori_loop(1, n_blk, start_sum, 0, unroll=few)
    lax.fori_loop(1, n_blk, wait_sum, 0, unroll=few)
    total = lax.fori_loop(
        0, n_blk, lambda i, total: total + parts[i], jnp.zeros(parts.shape[1:], jnp.float32), unroll=few
    )
    out_bank[...] = total[:, 0:count]
    out_pair[...] = total[0:out_pair.shape[0], count:count + lhs.shape[0]]

    for k, (distance, source, target) in enumerate(hops):
        goes = (me + distance < n_blk) if distance > 0 else (me + distance >= 0)

        @pl.when(goes)
        def _():
            halo(k, me).wait_send()

    for step in range(1, n_col):
        column_copy(step, mine, mine).wait_send()
    lax.fori_loop(1, n_blk, wait_sent, 0, unroll=few)


def local(n_blk, n_col, direct_init, adjoint_init, jacobian, areas, volumes, neighbours, block_cells, bank):
    fields, own, cell_count = direct_init.shape
    count = bank.shape[0]
    wide = fields * cell_count
    scale_norm = (fields * cell_count * n_blk) ** (-0.5)
    vmem = pl.BlockSpec(memory_space=pltpu.VMEM)
    f32 = jnp.float32
    dma = pltpu.SemaphoreType.DMA
    pair, projected = pl.pallas_call(
        functools.partial(kernel, n_blk, n_col, scale_norm),
        out_shape=(
            pltpu.VMEM((own, n_col * own), f32),
            pltpu.VMEM((n_col * own, count), f32),
        ),
        in_specs=[pl.BlockSpec(memory_space=pl.ANY)] * 8,
        out_specs=(vmem, vmem),
        scratch_shapes=[
            pltpu.VMEM((16, ROWS, LANES), f32),
            pltpu.VMEM((SLOTS + 1, fields, 8, LANES), f32),
            pltpu.VMEM((SLOTS + 1, fields, 8, LANES), f32),
            pltpu.VMEM((SLOTS, fields, 8, LANES), f32),
            pltpu.VMEM((SLOTS, 6, 8, LANES), f32),
            pltpu.VMEM((SLOTS, 6, 8, LANES), jnp.int32),
            pltpu.VMEM((SLOTS, 6, 8, LANES), jnp.int32),
            pltpu.VMEM((SLOTS, 8, LANES), f32),
            pltpu.VMEM((fields * fields, 8, LANES), f32),
            pltpu.VMEM((16, wide), f32),
            pltpu.VMEM((n_col, own, wide), jnp.bfloat16),
            pltpu.VMEM((n_blk, n_col * own, count + n_col * own), f32),
            pltpu.SMEM(jacobian.shape, f32),
            pltpu.SMEM(block_cells.shape, jnp.int32),
            pltpu.VMEM(direct_init.shape, f32),
            pltpu.VMEM(adjoint_init.shape, f32),
            pltpu.VMEM(areas.shape, f32),
            pltpu.VMEM((1, cell_count), f32),
            pltpu.VMEM(neighbours.shape, jnp.int32),
            pltpu.VMEM((fields, count, cell_count), jnp.bfloat16),
            dma((8,)),
            dma((6,)), dma((6,)), dma((n_col,)), dma((n_col,)), dma((n_blk,)), dma((n_blk,)),
        ],
        compiler_params=pltpu.CompilerParams(collective_id=0, has_side_effects=True),
        name="hankel",
    )(jacobian, block_cells, direct_init, adjoint_init, areas, volumes.reshape(1, cell_count), neighbours, bank.transpose(1, 0, 2))
    return pair.T, projected


def solution(mesh):
    return jax.shard_map(
        functools.partial(local, mesh.shape["blk"], mesh.shape["col"]),
        mesh=mesh,
        in_specs=(
            P(None, "col", "blk"),
            P(None, "col", "blk"),
            P(),
            P(None, "blk"),
            P("blk"),
            P(None, "blk"),
            P("blk"),
            P("col", None, "blk"),
        ),
        out_specs=(P(None, "col"), P(None, "col")),
        check_vma=False,
    )
```

```python
import functools

import jax
import jax.numpy as jnp
from jax import lax
from jax.experimental import pallas as pl
from jax.experimental.pallas import tpu as pltpu
from jax.sharding import PartitionSpec as P

STEPS = 3
TIME_STEP = 0.1
LANES = 128
ROWS = 32
SLOTS = 8
MESH = pl.DeviceIdType.MESH


def lane_take(values, index):
    return jnp.take_along_axis(values, index, axis=1, mode="promise_in_bounds")


def kernel(
    n_blk, n_col, scale_norm,
    jac_in, cells_in, direct_in, adjoint_in, areas_in, volumes_in, neighbours_in, bank_in,
    out_pair, out_bank,
    ext, state, middle, rates, coef, index, side, coef_sum, mixing, adj_rows, messages, parts,
    jac, cells, direct, adjoint, areas, volumes, neighbours, bank, loaded,
    halo_send, halo_recv, col_send, col_recv, sum_send, sum_recv,
):
    fields = direct.shape[0]
    tiles = direct.shape[2] // LANES
    me = lax.axis_index("blk")
    mine = lax.axis_index("col")

    loads = [
        pltpu.make_async_copy(source, target, loaded.at[k])
        for k, (source, target) in enumerate((
            (cells_in, cells), (direct_in, direct), (adjoint_in, adjoint), (areas_in, areas),
            (volumes_in, volumes), (neighbours_in, neighbours), (jac_in, jac), (bank_in, bank),
        ))
    ]
    for load in loads[:6]:
        load.start()

    barrier = pltpu.get_barrier_semaphore()

    def greet(axis, own, count):
        def one(step, carry):
            peer = lax.rem(own + step, count)
            pl.semaphore_signal(barrier, inc=1, device_id={axis: peer}, device_id_type=MESH)
            return carry
        lax.fori_loop(1, count, one, 0, unroll=count <= 16)

    greet("blk", me, n_blk)
    greet("col", mine, n_col)
    for load in loads[6:]:
        load.start()
    for load in loads[:6]:
        load.wait()

    lane = lax.broadcasted_iota(jnp.int32, (1, LANES), 1)
    for t in range(tiles):
        part = pl.ds(t * LANES, LANES)
        live = jnp.where(lane < cells[t], 1.0, 0.0)
        for g in range(fields):
            ext[6 + t, 4 * g:4 * g + 2, :] = direct[g, :, part] * live
            ext[6 + t, 4 * g + 2:4 * g + 4, :] = adjoint[g, :, part] * live
        ext[6 + t, 20:26, :] = live * areas[:, part] / volumes[:, part]
        ext[6 + t, 26:32, :] = neighbours[:, part].astype(jnp.float32)

    pl.semaphore_wait(barrier, n_blk - 1 + n_col - 1)

    hops = (
        (1, (8, 2), (4, 2)),
        (-1, (6, 2), (10, 2)),
        (1, (6, 2), (2, 2)),
        (-1, (8, 2), (12, 2)),
        (2, (8, 2), (0, 2)),
        (-2, (6, 2), (14, 2)),
    )

    def halo(k, peer):
        distance, source, target = hops[k]
        return pltpu.make_async_remote_copy(
            src_ref=ext.at[pl.ds(*source)],
            dst_ref=ext.at[pl.ds(*target)],
            send_sem=halo_send.at[k],
            recv_sem=halo_recv.at[k],
            device_id={"blk": peer},
            device_id_type=MESH,
        )

    for k, (distance, source, target) in enumerate(hops):
        goes = (me + distance < n_blk) if distance > 0 else (me + distance >= 0)

        @pl.when(goes)
        def _():
            halo(k, me + distance).start()

        comes = (me - distance >= 0) if distance > 0 else (me - distance < n_blk)

        @pl.when(jnp.logical_not(comes))
        def _():
            ext[pl.ds(*target)] = jnp.zeros((target[1], ROWS, LANES), jnp.float32)

    for load in loads[6:]:
        load.wait()
    sub = lax.broadcasted_iota(jnp.int32, (8, LANES), 0)
    is_direct = lax.rem(sub, 4) < 2
    for g in range(fields):
        for h in range(fields):
            mixing[g * fields + h] = jnp.where(is_direct, -jac[g, h], jac[h, g])
    span = tiles * LANES
    count = bank.shape[1]
    adj_rows[...] = jnp.zeros(adj_rows.shape, jnp.float32)

    def arrive(ids):
        for k in ids:
            distance = hops[k][0]
            comes = (me - distance >= 0) if distance > 0 else (me - distance < n_blk)

            @pl.when(comes)
            def _():
                halo(k, me).wait_recv()

    low = sub < 4

    def both(p, row):
        a = jnp.broadcast_to(ext[p, row:row + 1, :], (8, LANES))
        b = jnp.broadcast_to(ext[15 - p, row:row + 1, :], (8, LANES))
        return jnp.where(low, a, b)

    wide = lax.broadcasted_iota(jnp.int32, (8, LANES), 1)

    def unpack(p):
        for g in range(fields):
            state[p, g] = jnp.concatenate(
                [ext[p, 4 * g:4 * g + 4, :], ext[15 - p, 4 * g:4 * g + 4, :]], axis=0
            )
        if p == 0:
            return
        total = jnp.zeros((8, LANES), jnp.float32)
        for f in range(6):
            offset = both(p, 26 + f).astype(jnp.int32)
            c = both(p, 20 + f)
            total = total + c
            coef[p, f] = jnp.where(offset == 0, 0.0, c)
            target = wide + offset
            index[p, f] = jnp.bitwise_and(target, LANES - 1)
            way = jnp.where(target < 0, -1, jnp.where(target >= LANES, 1, 0))
            side[p, f] = jnp.where(low, way, -way)
        coef_sum[p] = total

    def swap_middle(buffer):
        for g in range(fields):
            buffer[SLOTS, g] = pltpu.roll(buffer[SLOTS - 1, g], 4, 0)

    def rate(buffer, p):
        even = [jnp.zeros((8, LANES), jnp.float32) for _ in range(fields)]
        odd = [jnp.zeros((8, LANES), jnp.float32) for _ in range(fields)]
        center = [buffer[p, g] for g in range(fields)]
        for f in range(6):
            ix = index[p, f]
            sd = side[p, f]
            c = coef[p, f]
            outer = sd < 0
            inner = sd > 0
            for g in range(fields):
                got = lane_take(center[g], ix)
                got = jnp.where(outer, lane_take(buffer[p - 1, g], ix), got)
                got = jnp.where(inner, lane_take(buffer[p + 1, g], ix), got)
                if f % 2 == 0:
                    even[g] = even[g] + c * got
                else:
                    odd[g] = odd[g] + c * got
        drift = [even[g] - odd[g] for g in range(fields)]
        result = []
        for g in range(fields):
            value = even[g] + odd[g] - coef_sum[p] * center[g]
            for h in range(fields):
                value = value + mixing[g * fields + h] * drift[h]
            result.append(value)
        return center, result

    def advance(stage, p):
        if stage % 2:
            center, value = rate(state, p)
            for g in range(fields):
                rates[p, g] = value[g]
                middle[p, g] = center[g] + TIME_STEP * value[g]
        else:
            _, value = rate(middle, p)
            for g in range(fields):
                state[p, g] = state[p, g] + (0.5 * TIME_STEP) * (rates[p, g] + value[g])
        if p == SLOTS - 1 and stage < 2 * STEPS:
            swap_middle(middle if stage % 2 else state)

    weights = []
    for t in range(tiles):
        live = jnp.where(lane < cells[t], 1.0, 0.0)
        weights.append(volumes[:, t * LANES:(t + 1) * LANES] * live * scale_norm)
    lowest, done = SLOTS, {stage: SLOTS for stage in range(1, 2 * STEPS + 1)}
    for bottom, ids in ((6, ()), (4, (0, 1)), (0, (2, 3, 4, 5))):
        arrive(ids)
        for p in range(lowest - 1, bottom - 1, -1):
            unpack(p)
        if lowest == SLOTS:
            swap_middle(state)
        lowest = bottom
        for stage in range(1, 2 * STEPS + 1):
            start = min(bottom + stage, SLOTS)
            for p in range(start, done[stage]):
                advance(stage, p)
            done[stage] = start

    direct_rows = []
    for g in range(fields):
        for t in range(tiles):
            e = 6 + t
            p, row = (e, 0) if e < SLOTS else (15 - e, 4)
            column = pl.ds(g * span + t * LANES, LANES)
            direct_rows.append(weights[t] * state[p, g, row:row + 2, :])
            adj_rows[0:2, column] = state[p, g, row + 2:row + 4, :]
    messages[mine] = jnp.concatenate(direct_rows, axis=1).astype(jnp.bfloat16)

    def column_copy(step, slot, peer):
        return pltpu.make_async_remote_copy(
            src_ref=messages.at[slot],
            dst_ref=messages.at[slot],
            send_sem=col_send.at[step],
            recv_sem=col_recv.at[slot],
            device_id={"col": peer},
            device_id_type=MESH,
        )

    for step in range(1, n_col):
        column_copy(step, mine, lax.rem(mine + step, n_col)).start()
    own_adjoint = adj_rows[...].astype(jnp.bfloat16)
    for step in range(1, n_col):
        slot = lax.rem(mine + step, n_col)
        column_copy(step, slot, slot).wait_recv()

    lhs = jnp.concatenate(
        [messages[c].astype(jnp.float32) for c in range(n_col)], axis=0
    ).astype(jnp.bfloat16)
    contract = (((1,), (1,)), ((), ()))
    bank_part = jnp.zeros((lhs.shape[0], count), jnp.float32)
    for g in range(fields):
        bank_part = bank_part + lax.dot_general(
            lhs[:, g * span:(g + 1) * span], bank[g], contract, preferred_element_type=jnp.float32
        )
    pair_part = lax.dot_general(own_adjoint, lhs, contract, preferred_element_type=jnp.float32)
    parts[me] = jnp.concatenate([bank_part, pair_part[0:8]], axis=1)

    def sum_copy(step, slot, peer):
        return pltpu.make_async_remote_copy(
            src_ref=parts.at[slot],
            dst_ref=parts.at[slot],
            send_sem=sum_send.at[step],
            recv_sem=sum_recv.at[slot],
            device_id={"blk": peer},
            device_id_type=MESH,
        )

    def start_sum(step, carry):
        sum_copy(step, me, lax.rem(me + step, n_blk)).start()
        return carry

    def wait_sum(step, carry):
        slot = lax.rem(me + step, n_blk)
        sum_copy(step, slot, slot).wait_recv()
        return carry

    def wait_sent(step, carry):
        sum_copy(step, me, lax.rem(me + step, n_blk)).wait_send()
        return carry

    few = n_blk <= 16
    if few:
        for step in sorted(range(1, n_blk), key=lambda i: -min(i, n_blk - i)):
            start_sum(step, 0)
    else:
        lax.fori_loop(1, n_blk, start_sum, 0)
    lax.fori_loop(1, n_blk, wait_sum, 0, unroll=few)
    total = lax.fori_loop(
        0, n_blk, lambda i, total: total + parts[i], jnp.zeros(parts.shape[1:], jnp.float32), unroll=few
    )
    out_bank[...] = total[:, 0:count]
    out_pair[...] = total[0:out_pair.shape[0], count:count + lhs.shape[0]]

    for k, (distance, source, target) in enumerate(hops):
        goes = (me + distance < n_blk) if distance > 0 else (me + distance >= 0)

        @pl.when(goes)
        def _():
            halo(k, me).wait_send()

    for step in range(1, n_col):
        column_copy(step, mine, mine).wait_send()
    lax.fori_loop(1, n_blk, wait_sent, 0, unroll=few)


def local(n_blk, n_col, direct_init, adjoint_init, jacobian, areas, volumes, neighbours, block_cells, bank):
    fields, own, cell_count = direct_init.shape
    count = bank.shape[0]
    wide = fields * cell_count
    scale_norm = (fields * cell_count * n_blk) ** (-0.5)
    vmem = pl.BlockSpec(memory_space=pltpu.VMEM)
    f32 = jnp.float32
    dma = pltpu.SemaphoreType.DMA
    pair, projected = pl.pallas_call(
        functools.partial(kernel, n_blk, n_col, scale_norm),
        out_shape=(
            pltpu.VMEM((own, n_col * own), f32),
            pltpu.VMEM((n_col * own, count), f32),
        ),
        in_specs=[pl.BlockSpec(memory_space=pl.ANY)] * 8,
        out_specs=(vmem, vmem),
        scratch_shapes=[
            pltpu.VMEM((16, ROWS, LANES), f32),
            pltpu.VMEM((SLOTS + 1, fields, 8, LANES), f32),
            pltpu.VMEM((SLOTS + 1, fields, 8, LANES), f32),
            pltpu.VMEM((SLOTS, fields, 8, LANES), f32),
            pltpu.VMEM((SLOTS, 6, 8, LANES), f32),
            pltpu.VMEM((SLOTS, 6, 8, LANES), jnp.int32),
            pltpu.VMEM((SLOTS, 6, 8, LANES), jnp.int32),
            pltpu.VMEM((SLOTS, 8, LANES), f32),
            pltpu.VMEM((fields * fields, 8, LANES), f32),
            pltpu.VMEM((16, wide), f32),
            pltpu.VMEM((n_col, own, wide), jnp.bfloat16),
            pltpu.VMEM((n_blk, n_col * own, count + n_col * own), f32),
            pltpu.SMEM(jacobian.shape, f32),
            pltpu.SMEM(block_cells.shape, jnp.int32),
            pltpu.VMEM(direct_init.shape, f32),
            pltpu.VMEM(adjoint_init.shape, f32),
            pltpu.VMEM(areas.shape, f32),
            pltpu.VMEM((1, cell_count), f32),
            pltpu.VMEM(neighbours.shape, jnp.int32),
            pltpu.VMEM((fields, count, cell_count), jnp.bfloat16),
            dma((8,)),
            dma((6,)), dma((6,)), dma((n_col,)), dma((n_col,)), dma((n_blk,)), dma((n_blk,)),
        ],
        compiler_params=pltpu.CompilerParams(collective_id=0, has_side_effects=True),
        name="hankel",
    )(jacobian, block_cells, direct_init, adjoint_init, areas, volumes.reshape(1, cell_count), neighbours, bank.transpose(1, 0, 2))
    return pair.T, projected


def solution(mesh):
    return jax.shard_map(
        functools.partial(local, mesh.shape["blk"], mesh.shape["col"]),
        mesh=mesh,
        in_specs=(
            P(None, "col", "blk"),
            P(None, "col", "blk"),
            P(),
            P(None, "blk"),
            P("blk"),
            P(None, "blk"),
            P("blk"),
            P("col", None, "blk"),
        ),
        out_specs=(P(None, "col"), P(None, "col")),
        check_vma=False,
    )
```
